32 devices in a mesh: parts: 2 (over y), blk: 16 (over z, x, core).
Axes of the slice: x: 2, y: 2, z: 4, core: 2. Of those that a mesh axis runs over, the one named last changes fastest.
Arguments:
- series: bfloat16 [16, 192, 11264], P(None, None, 'blk'), may hold values from -24 to 24
- subject_ids: int32 [16], P('parts'), parts along dimension 0, may hold values from 0 to 15
- net_labels: int32 [16], replicated, may hold values from 0 to 6
Outputs:
- connectome: float32 [22528, 11264], P(('parts', 'blk')), parts along dimension 0
The draws below stay inside these ranges and needn't reach their ends.
There are 2 independent parts, one for each index of `parts`. The reference program is written for one: setup_inputs(seed, part) draws one part's arguments, and reference() takes and returns one part's arrays. A program takes and returns all parts, laid end to end along the dimension named above; an argument that names none is the same for every part. Nothing has to cross between parts.
Inputs may be any that keep to these rules, and one draw needn't show every extreme that they name: `subject_ids`: indices into the pool; a subject may repeat.
All inputs are finite; a program needn't handle non-finite values.
Results may differ from the reference program's by a relative error of at most 0.00072.
Values may be sent and summed in bfloat16 or wider, within the bound.
A program may use at most 384 MiB of HBM per device.

```python
import math
import jax
import jax.numpy as jnp
import numpy as np
from jax import lax

BLOCK = 704
NBLOCK = 16
NET = 7
SUBJ = 8
POOL = 16
FRAMES = 192
G = 11264


def draw_series(key, part):
    keys = jax.random.split(key, 4)
    own = jax.random.truncated_normal(keys[0], -4.0, 4.0, (POOL, FRAMES, NBLOCK), jnp.float32)
    common = jax.random.truncated_normal(keys[1], -4.0, 4.0, (POOL, FRAMES, 1), jnp.float32)
    latent = jnp.repeat(own + 0.7 * common, BLOCK, axis=2)
    loading = jax.random.uniform(keys[2], (POOL, 1, G), jnp.float32, 0.8, 2.5)
    noise = jax.random.truncated_normal(keys[3], -4.0, 4.0, (POOL, FRAMES, G), jnp.float32)
    values = loading * latent + noise
    return values.astype(jnp.bfloat16)


def with_ends(values, key, least, largest):
    extent = values.shape
    place = [jax.random.randint(jax.random.fold_in(key, axis), (), 0, extent[axis]) for axis in range(len(extent))]
    values = values.at[tuple(place)].set(least)
    longest = extent.index(max(extent))
    place[longest] = (place[longest] + 1) % extent[longest]
    return values.at[tuple(place)].set(largest)


def rank_bounds(count, lean):
    portions = [(1 << 20) // math.isqrt(standing ** lean) + 1 for standing in range(1, count + 1)]
    scale = 1 + sum(portions) // (1 << 30)
    return np.cumsum(np.array([max(1, weight // scale) for weight in portions]))


def skewed_ids(stream_key, shape, count, skew):
    grid = rank_bounds(count, skew)
    pick = jax.random.randint(jax.random.fold_in(stream_key, 1), shape, 0, int(grid[count - 1]))
    rank = jnp.searchsorted(jnp.asarray(grid, jnp.int32), pick, side="right")
    return jax.random.permutation(jax.random.fold_in(stream_key, 2), count)[rank].astype(jnp.int32)


def setup_inputs(seed: int = 0, part: int = 0) -> dict:
    streams_of = jax.random.split(jax.random.key(seed), 4)
    part_keys = jax.random.split(jax.random.fold_in(streams_of[3], part), 4)
    return {
        "series": draw_series(jax.random.fold_in(streams_of[3], 71), part),
        "subject_ids": with_ends(jax.random.randint(part_keys[1], (SUBJ,), 0, POOL), jax.random.fold_in(part_keys[1], 1), 0, POOL - 1).astype(jnp.int32),
        "net_labels": with_ends(skewed_ids(streams_of[2], (NBLOCK,), NET, 2), jax.random.fold_in(streams_of[2], 3), 0, NET - 1).astype(jnp.int32),
    }


def fisher_value(corr):
    clipped = jnp.clip(corr, -0.999, 0.999)
    return 0.5 * jnp.log((1.0 + clipped) / (1.0 - clipped))

def reference(series, subject_ids, net_labels):
    chosen = series[subject_ids].astype(jnp.float32)
    center = chosen - lax.optimization_barrier(jnp.mean(chosen, axis=1, keepdims=True))
    spread = lax.optimization_barrier(jnp.mean(center * center, axis=1, keepdims=True))
    normalized = (center / jnp.sqrt(spread + 1e-05)).astype(jnp.bfloat16)
    row_labels = jnp.repeat(net_labels, BLOCK)
    blocks = normalized.reshape(SUBJ, FRAMES, NBLOCK, BLOCK).transpose(2, 0, 1, 3)

    def one_block(inputs):
        block_rows, label = inputs
        total = jnp.zeros((BLOCK, G), jnp.float32)
        for subject in range(SUBJ):
            corr = jnp.dot(block_rows[subject].T, normalized[subject], preferred_element_type=jnp.float32) / FRAMES
            total = total + fisher_value(corr)
        return jnp.where(label == row_labels[None, :], total, jnp.zeros_like(total))
    result = lax.map(one_block, (blocks, net_labels))
    return result.reshape(G, G)
```

```python
import functools
import math

import jax
import jax.numpy as jnp
from jax import lax
from jax.experimental import pallas as pl
from jax.experimental.pallas import tpu as pltpu
from jax.sharding import PartitionSpec as P

USE_KERNEL_GATHER = True
LIMIT = 0.999


def normalize(chosen):
    values = chosen.astype(jnp.float32)
    center = values - jnp.mean(values, axis=1, keepdims=True)
    spread = jnp.mean(center * center, axis=1, keepdims=True)
    return (center / jnp.sqrt(spread + 1e-05)).astype(jnp.bfloat16)


def fisher_sum(left, right):
    frames = left.shape[1]
    total = jnp.zeros((left.shape[2], right.shape[2]), jnp.float32)
    for subject in range(left.shape[0]):
        corr = (
            lax.dot_general(
                left[subject],
                right[subject],
                (((0,), (0,)), ((), ())),
                preferred_element_type=jnp.float32,
            )
            / frames
        )
        clipped = jnp.clip(corr, -LIMIT, LIMIT)
        total = total + 0.5 * jnp.log((1.0 + clipped) / (1.0 - clipped))
    return total


def plain(series, subject_ids, net_labels):
    normalized = normalize(jnp.take(series, subject_ids, axis=0))
    rows = normalized.shape[2]
    index = lax.axis_index("blk")
    count = lax.axis_size("blk")
    row_labels = jnp.repeat(net_labels, count * rows // net_labels.shape[0])
    own_labels = lax.dynamic_slice_in_dim(row_labels, index * rows, rows)
    gathered = lax.all_gather(normalized, "blk", axis=2, tiled=True)
    same = own_labels[:, None] == row_labels[None, :]
    return jnp.where(same, fisher_sum(normalized, gathered), 0.0)


def normalize_kernel(ids_ref, me_ref, series_ref, out_ref, turned_ref):
    values = series_ref[0].astype(jnp.float32)
    frames = values.shape[0]
    center = values - jnp.sum(values, axis=0, keepdims=True) / frames
    spread = jnp.sum(center * center, axis=0, keepdims=True) / frames
    result = center / jnp.sqrt(spread + 1e-05)
    out_ref[0, 0] = result.astype(jnp.bfloat16)
    turned_ref[0] = result.T.astype(jnp.bfloat16)


def normalized_blocks(series, subject_ids, me, slots):
    _, frames, width = series.shape
    subjects = subject_ids.shape[0]
    return pl.pallas_call(
        normalize_kernel,
        grid_spec=pltpu.PrefetchScalarGridSpec(
            num_scalar_prefetch=2,
            grid=(subjects,),
            in_specs=[pl.BlockSpec((1, frames, width), lambda s, ids, me: (ids[s], 0, 0))],
            out_specs=[
                pl.BlockSpec((1, 1, frames, width), lambda s, ids, me: (me[0], s, 0, 0)),
                pl.BlockSpec((1, width, frames), lambda s, ids, me: (s, 0, 0)),
            ],
        ),
        out_shape=[
            jax.ShapeDtypeStruct((slots, subjects, frames, width), jnp.bfloat16),
            jax.ShapeDtypeStruct((subjects, width, frames), jnp.bfloat16),
        ],
        name="normalize",
    )(subject_ids, me, series)


def gather_kernel(count, chunks, in_ref, out_ref, send_sem, recv_sem):
    tall = count // 4
    me = lax.axis_index("blk")
    z = me // 4
    x = (me // 2) % 2
    c = me % 2
    per = out_ref.shape[1] // chunks
    UP, DOWN, SIDE, TWIN = range(4)
    half = chunks // 2

    def device(zz, xx, cc):
        return (zz * 2 + xx) * 2 + cc

    target = {
        UP: device(jnp.minimum(z + 1, tall - 1), x, c),
        DOWN: device(jnp.maximum(z - 1, 0), x, c),
        SIDE: device(z, 1 - x, c),
        TWIN: device(z, x, 1 - c),
    }
    has_up, has_down = z + 1 < tall, z > 0

    barrier = pltpu.get_barrier_semaphore()

    def greet(way):
        pl.semaphore_signal(
            barrier, inc=1, device_id={"blk": target[way]}, device_id_type=pl.DeviceIdType.MESH
        )

    greet(SIDE)
    greet(TWIN)
    pl.when(has_up)(lambda: greet(UP))
    pl.when(has_down)(lambda: greet(DOWN))
    pl.semaphore_wait(barrier, 2 + has_up.astype(jnp.int32) + has_down.astype(jnp.int32))

    def copy(way, block, q):
        part = out_ref.at[block, pl.ds(q * per, per)]
        return pltpu.make_async_remote_copy(
            src_ref=part,
            dst_ref=part,
            send_sem=send_sem.at[way, block, q],
            recv_sem=recv_sem.at[block, q],
            device_id={"blk": target[way]},
            device_id_type=pl.DeviceIdType.MESH,
        )

    def send(way, block, q):
        copy(way, block, q).start()

    def arrived(block, q):
        copy(TWIN, block, q).wait_recv()

    def by_side(zz, at, q):
        if q < half:
            return jnp.bool_(True)
        low = jnp.logical_and(zz == 0, at > 0)
        high = jnp.logical_and(zz == tall - 1, at < tall - 1)
        return jnp.logical_not(jnp.logical_or(low, high))

    for q in range(chunks):
        pl.when(has_up)(lambda: send(UP, me, q))
        pl.when(has_down)(lambda: send(DOWN, me, q))
        pl.when(by_side(z, z, q))(lambda: send(SIDE, me, q))
        send(TWIN, me, q)

    def step(k, carry):
        for q in range(chunks):

            @pl.when(z - k >= 0)
            def _():
                block = device(z - k, x, c)
                arrived(block, q)
                pl.when(has_up)(lambda: send(UP, block, q))
                pl.when(by_side(z - k, z, q))(lambda: send(SIDE, block, q))
                send(TWIN, block, q)

            @pl.when(z + k < tall)
            def _():
                block = device(z + k, x, c)
                arrived(block, q)
                pl.when(has_down)(lambda: send(DOWN, block, q))
                pl.when(by_side(z + k, z, q))(lambda: send(SIDE, block, q))
                send(TWIN, block, q)

            if q >= half:

                @pl.when(jnp.logical_and(z - k == -1, has_down))
                def _():
                    block = device(0, 1 - x, c)
                    arrived(block, q)
                    pl.when(has_up)(lambda: send(UP, block, q))
                    send(TWIN, block, q)

                @pl.when(jnp.logical_and(z + k == tall, has_up))
                def _():
                    block = device(tall - 1, 1 - x, c)
                    arrived(block, q)
                    pl.when(has_down)(lambda: send(DOWN, block, q))
                    send(TWIN, block, q)

            @pl.when(k == 1)
            def _():
                block = device(z, 1 - x, c)
                arrived(block, q)
                if q >= half:
                    pl.when(jnp.logical_and(z == 0, has_up))(lambda: send(UP, block, q))
                    pl.when(jnp.logical_and(z == tall - 1, has_down))(lambda: send(DOWN, block, q))
                send(TWIN, block, q)

            low = z - k + 1

            @pl.when(jnp.logical_and(jnp.logical_and(k > 1, low >= 0), by_side(low, z, q)))
            def _():
                block = device(low, 1 - x, c)
                arrived(block, q)
                send(TWIN, block, q)

            high = z + k - 1

            @pl.when(jnp.logical_and(jnp.logical_and(k > 1, high < tall), by_side(high, z, q)))
            def _():
                block = device(high, 1 - x, c)
                arrived(block, q)
                send(TWIN, block, q)

        return carry

    lax.fori_loop(1, tall + 1, step, 0)

    def finish(zz, carry):
        for q in range(chunks):
            own = device(zz, x, c)
            other = device(zz, 1 - x, c)
            arrived(device(zz, x, 1 - c), q)
            arrived(device(zz, 1 - x, 1 - c), q)
            copy(TWIN, own, q).wait_send()
            copy(TWIN, other, q).wait_send()
            pl.when(by_side(zz, z, q))(lambda: copy(SIDE, own, q).wait_send())
            pl.when(jnp.logical_and(has_up, zz <= z))(lambda: copy(UP, own, q).wait_send())
            pl.when(jnp.logical_and(has_down, zz >= z))(lambda: copy(DOWN, own, q).wait_send())
            if q >= half:
                pl.when(jnp.logical_and(has_up, zz == 0))(
                    lambda: copy(UP, other, q).wait_send()
                )
                pl.when(jnp.logical_and(has_down, zz == tall - 1))(
                    lambda: copy(DOWN, other, q).wait_send()
                )
        return carry

    lax.fori_loop(0, tall, finish, 0)


def gather(blocks, count):
    subjects = blocks.shape[1]
    chunks = math.gcd(subjects, 4)
    return pl.pallas_call(
        functools.partial(gather_kernel, count, chunks),
        out_shape=jax.ShapeDtypeStruct(blocks.shape, blocks.dtype),
        in_specs=[pl.BlockSpec(memory_space=pl.ANY)],
        out_specs=pl.BlockSpec(memory_space=pl.ANY),
        scratch_shapes=[
            pltpu.SemaphoreType.DMA((4, count, chunks)),
            pltpu.SemaphoreType.DMA((count, chunks)),
        ],
        input_output_aliases={0: 0},
        compiler_params=pltpu.CompilerParams(collective_id=0, has_side_effects=True),
        name="gather",
    )(blocks)


def fisher_kernel(rows, group, fetch_ref, match_ref, left_ref, right_ref, out_ref, pair):
    step = pl.program_id(0)
    subjects, width, frames = left_ref.shape
    first, second = match_ref[2 * step], match_ref[2 * step + 1]
    low = width // 128 * 128
    high = (width + 127) // 128 * 128
    bound = LIMIT * frames

    @pl.when(first + second == 0)
    def _():
        out_ref[...] = jnp.zeros_like(out_ref)

    @pl.when(first + second > 0)
    def _():
        for s in range(subjects):
            pair[s, :, :width] = right_ref[0, s]
            pair[s, :, width:] = right_ref[1, s]

    def tile(start, size, wanted, mixed):
        @pl.when(jnp.logical_and(wanted == 0, first + second > 0))
        def _():
            out_ref[:, start : start + size] = jnp.zeros((width, size), jnp.float32)

        @pl.when(wanted > 0)
        def _():
            def body(r, carry):
                at = pl.ds(pl.multiple_of(r * rows, rows), rows)
                total = None
                for g in range(0, subjects, group):
                    over = under = None
                    for s in range(g, min(g + group, subjects)):
                        dot = jnp.dot(
                            left_ref[s, at, :],
                            pair[s, :, start : start + size],
                            preferred_element_type=jnp.float32,
                        )
                        dot = jnp.clip(dot, -bound, bound)
                        plus, minus = frames + dot, frames - dot
                        over = plus if over is None else over * plus
                        under = minus if under is None else under * minus
                    term = 0.5 * jnp.log(over / under)
                    total = term if total is None else total + term
                if mixed:
                    lane = start + lax.broadcasted_iota(jnp.int32, total.shape, 1)
                    keep = jnp.where(lane < width, first, second)
                    total = jnp.where(keep > 0, total, 0.0)
                out_ref[at, start : start + size] = total
                return carry

            lax.fori_loop(0, width // rows, body, 0)

    for start in range(0, low, 256):
        tile(start, min(256, low - start), first, False)
    if high > low:
        tile(low, high - low, first + second, True)
    for start in range(high, 2 * width, 256):
        tile(start, min(256, 2 * width - start), second, False)


def correlate(left, blocks, match):
    count, subjects, frames, width = blocks.shape
    pairs = count // 2
    wanted = jnp.max(match.reshape(pairs, 2), axis=1)
    index = jnp.arange(pairs)
    latest = jnp.max(jnp.where((index[None, :] <= index[:, None]) & (wanted[None, :] > 0), index[None, :], 0), axis=1)
    group = max(1, int(30 / math.log10(2 * frames)))
    rows = math.gcd(width, 64)
    return pl.pallas_call(
        functools.partial(fisher_kernel, rows, group),
        grid_spec=pltpu.PrefetchScalarGridSpec(
            num_scalar_prefetch=2,
            grid=(pairs,),
            in_specs=[
                pl.BlockSpec((subjects, width, frames), lambda p, fetch, match: (0, 0, 0)),
                pl.BlockSpec((2, subjects, frames, width), lambda p, fetch, match: (fetch[p], 0, 0, 0)),
            ],
            out_specs=pl.BlockSpec((width, 2 * width), lambda p, fetch, match: (0, p)),
            scratch_shapes=[pltpu.VMEM((subjects, frames, 2 * width), jnp.bfloat16)],
        ),
        out_shape=jax.ShapeDtypeStruct((width, count * width), jnp.float32),
        compiler_params=pltpu.CompilerParams(vmem_limit_bytes=60 * 1024 * 1024),
        name="correlate",
    )(latest.astype(jnp.int32), match, left, blocks)


def on_device(series, subject_ids, net_labels):
    count = lax.axis_size("blk")
    width = series.shape[2]
    fits = net_labels.shape[0] == count and count % 4 == 0 and 2 * width % 128 == 0
    if not fits:
        return plain(series, subject_ids, net_labels)
    me = lax.axis_index("blk").astype(jnp.int32)
    match = (net_labels == net_labels[me]).astype(jnp.int32)
    if USE_KERNEL_GATHER:
        blocks, left = normalized_blocks(series, subject_ids, me[None], count)
        blocks = gather(blocks, count)
    else:
        own, left = normalized_blocks(series, subject_ids, jnp.zeros((1,), jnp.int32), 1)
        blocks = lax.all_gather(own, "blk", axis=0, tiled=True)
    return correlate(left, blocks, match)


def solution(mesh):
    return jax.shard_map(
        on_device,
        mesh=mesh,
        in_specs=(P(None, None, "blk"), P("parts"), P()),
        out_specs=P(("parts", "blk"), None),
        check_vma=False,
    )
```

```python
import functools
import math

import jax
import jax.numpy as jnp
from jax import lax
from jax.experimental import pallas as pl
from jax.experimental.pallas import tpu as pltpu
from jax.sharding import PartitionSpec as P

LIMIT = 0.999
LANES = 128
HALF = LANES // 2


def normalize(chosen):
    values = chosen.astype(jnp.float32)
    center = values - jnp.mean(values, axis=1, keepdims=True)
    spread = jnp.mean(center * center, axis=1, keepdims=True)
    return (center / jnp.sqrt(spread + 1e-05)).astype(jnp.bfloat16)


def fisher_sum(left, right):
    frames = left.shape[1]
    total = jnp.zeros((left.shape[2], right.shape[2]), jnp.float32)
    for subject in range(left.shape[0]):
        corr = (
            lax.dot_general(
                left[subject],
                right[subject],
                (((0,), (0,)), ((), ())),
                preferred_element_type=jnp.float32,
            )
            / frames
        )
        clipped = jnp.clip(corr, -LIMIT, LIMIT)
        total = total + 0.5 * jnp.log((1.0 + clipped) / (1.0 - clipped))
    return total


def plain(series, subject_ids, net_labels):
    normalized = normalize(jnp.take(series, subject_ids, axis=0))
    rows = normalized.shape[2]
    index = lax.axis_index("blk")
    count = lax.axis_size("blk")
    row_labels = jnp.repeat(net_labels, count * rows // net_labels.shape[0])
    own_labels = lax.dynamic_slice_in_dim(row_labels, index * rows, rows)
    gathered = lax.all_gather(normalized, "blk", axis=2, tiled=True)
    same = own_labels[:, None] == row_labels[None, :]
    return jnp.where(same, fisher_sum(normalized, gathered), 0.0)


def normalize_kernel(ids_ref, me_ref, series_ref, out_ref, turned_ref):
    values = series_ref[0].astype(jnp.float32)
    frames = values.shape[0]
    center = values - jnp.sum(values, axis=0, keepdims=True) / frames
    spread = jnp.sum(center * center, axis=0, keepdims=True) / frames
    result = center / jnp.sqrt(spread + 1e-05)
    turned_ref[0] = result.T.astype(jnp.bfloat16)
    packed = result.astype(jnp.bfloat16)
    width = packed.shape[1]
    tiles, top = width // LANES, frames // 2

    def pack(first, edge, upper, lower):
        for t in range(tiles):
            start = first + t * LANES
            out_ref[0, 0, t * frames : (t + 1) * frames, :] = packed[:, start : start + LANES]
        ends = {upper: packed[:top, edge : edge + HALF], lower: packed[top:, edge : edge + HALF]}
        out_ref[0, 0, tiles * frames :, :] = jnp.concatenate([ends[0], ends[1]], axis=1)

    pl.when(me_ref[0] % 2 == 0)(lambda: pack(0, tiles * LANES, 0, 1))
    pl.when(me_ref[0] % 2 == 1)(lambda: pack(HALF, 0, 1, 0))


def normalized_blocks(series, subject_ids, me, slots):
    _, frames, width = series.shape
    depth = width * frames // LANES
    subjects = subject_ids.shape[0]
    return pl.pallas_call(
        normalize_kernel,
        grid_spec=pltpu.PrefetchScalarGridSpec(
            num_scalar_prefetch=2,
            grid=(subjects,),
            in_specs=[pl.BlockSpec((1, frames, width), lambda s, ids, me: (ids[s], 0, 0))],
            out_specs=[
                pl.BlockSpec((1, 1, depth, LANES), lambda s, ids, me: (me[0], s, 0, 0)),
                pl.BlockSpec((1, width, frames), lambda s, ids, me: (s, 0, 0)),
            ],
        ),
        out_shape=[
            jax.ShapeDtypeStruct((slots, subjects, depth, LANES), jnp.bfloat16),
            jax.ShapeDtypeStruct((subjects, width, frames), jnp.bfloat16),
        ],
        name="normalize",
    )(subject_ids, me, series)


def gather_kernel(count, chunks, in_ref, out_ref, send_sem, recv_sem):
    tall = count // 4
    me = lax.axis_index("blk")
    z = me // 4
    x = (me // 2) % 2
    c = me % 2
    per = out_ref.shape[1] // chunks
    UP, DOWN, SIDE, TWIN = range(4)
    half = chunks // 2

    def device(zz, xx, cc):
        return (zz * 2 + xx) * 2 + cc

    target = {
        UP: device(jnp.minimum(z + 1, tall - 1), x, c),
        DOWN: device(jnp.maximum(z - 1, 0), x, c),
        SIDE: device(z, 1 - x, c),
        TWIN: device(z, x, 1 - c),
    }
    has_up, has_down = z + 1 < tall, z > 0

    barrier = pltpu.get_barrier_semaphore()

    def greet(way):
        pl.semaphore_signal(
            barrier, inc=1, device_id={"blk": target[way]}, device_id_type=pl.DeviceIdType.MESH
        )

    greet(SIDE)
    greet(TWIN)
    pl.when(has_up)(lambda: greet(UP))
    pl.when(has_down)(lambda: greet(DOWN))
    pl.semaphore_wait(barrier, 2 + has_up.astype(jnp.int32) + has_down.astype(jnp.int32))

    def copy(way, block, q):
        part = out_ref.at[block, pl.ds(q * per, per)]
        return pltpu.make_async_remote_copy(
            src_ref=part,
            dst_ref=part,
            send_sem=send_sem.at[way, block, q],
            recv_sem=recv_sem.at[block, q],
            device_id={"blk": target[way]},
            device_id_type=pl.DeviceIdType.MESH,
        )

    def send(way, block, q):
        copy(way, block, q).start()

    def arrived(block, q):
        copy(TWIN, block, q).wait_recv()

    def by_side(zz, at, q):
        if q < half:
            return jnp.bool_(True)
        low = jnp.logical_and(zz == 0, at > 0)
        high = jnp.logical_and(zz == tall - 1, at < tall - 1)
        return jnp.logical_not(jnp.logical_or(low, high))

    for q in range(chunks):
        pl.when(has_up)(lambda: send(UP, me, q))
        pl.when(has_down)(lambda: send(DOWN, me, q))
        pl.when(by_side(z, z, q))(lambda: send(SIDE, me, q))
        send(TWIN, me, q)

    def step(k, carry):
        for q in range(chunks):

            @pl.when(z - k >= 0)
            def _():
                block = device(z - k, x, c)
                arrived(block, q)
                pl.when(has_up)(lambda: send(UP, block, q))
                pl.when(by_side(z - k, z, q))(lambda: send(SIDE, block, q))
                send(TWIN, block, q)

            @pl.when(z + k < tall)
            def _():
                block = device(z + k, x, c)
                arrived(block, q)
                pl.when(has_down)(lambda: send(DOWN, block, q))
                pl.when(by_side(z + k, z, q))(lambda: send(SIDE, block, q))
                send(TWIN, block, q)

            if q >= half:

                @pl.when(jnp.logical_and(z - k == -1, has_down))
                def _():
                    block = device(0, 1 - x, c)
                    arrived(block, q)
                    pl.when(has_up)(lambda: send(UP, block, q))
                    send(TWIN, block, q)

                @pl.when(jnp.logical_and(z + k == tall, has_up))
                def _():
                    block = device(tall - 1, 1 - x, c)
                    arrived(block, q)
                    pl.when(has_down)(lambda: send(DOWN, block, q))
                    send(TWIN, block, q)

            @pl.when(k == 1)
            def _():
                block = device(z, 1 - x, c)
                arrived(block, q)
                if q >= half:
                    pl.when(jnp.logical_and(z == 0, has_up))(lambda: send(UP, block, q))
                    pl.when(jnp.logical_and(z == tall - 1, has_down))(lambda: send(DOWN, block, q))
                send(TWIN, block, q)

            low = z - k + 1

            @pl.when(jnp.logical_and(jnp.logical_and(k > 1, low >= 0), by_side(low, z, q)))
            def _():
                block = device(low, 1 - x, c)
                arrived(block, q)
                send(TWIN, block, q)

            high = z + k - 1

            @pl.when(jnp.logical_and(jnp.logical_and(k > 1, high < tall), by_side(high, z, q)))
            def _():
                block = device(high, 1 - x, c)
                arrived(block, q)
                send(TWIN, block, q)

        return carry

    lax.fori_loop(1, tall + 1, step, 0)

    def finish(zz, carry):
        for q in range(chunks):
            own = device(zz, x, c)
            other = device(zz, 1 - x, c)
            arrived(device(zz, x, 1 - c), q)
            arrived(device(zz, 1 - x, 1 - c), q)
            copy(TWIN, own, q).wait_send()
            copy(TWIN, other, q).wait_send()
            pl.when(by_side(zz, z, q))(lambda: copy(SIDE, own, q).wait_send())
            pl.when(jnp.logical_and(has_up, zz <= z))(lambda: copy(UP, own, q).wait_send())
            pl.when(jnp.logical_and(has_down, zz >= z))(lambda: copy(DOWN, own, q).wait_send())
            if q >= half:
                pl.when(jnp.logical_and(has_up, zz == 0))(
                    lambda: copy(UP, other, q).wait_send()
                )
                pl.when(jnp.logical_and(has_down, zz == tall - 1))(
                    lambda: copy(DOWN, other, q).wait_send()
                )
        return carry

    lax.fori_loop(0, tall, finish, 0)


def gather(blocks, count):
    subjects = blocks.shape[1]
    chunks = math.gcd(subjects, 4)
    return pl.pallas_call(
        functools.partial(gather_kernel, count, chunks),
        out_shape=jax.ShapeDtypeStruct(blocks.shape, blocks.dtype),
        in_specs=[pl.BlockSpec(memory_space=pl.ANY)],
        out_specs=pl.BlockSpec(memory_space=pl.ANY),
        scratch_shapes=[
            pltpu.SemaphoreType.DMA((4, count, chunks)),
            pltpu.SemaphoreType.DMA((count, chunks)),
        ],
        input_output_aliases={0: 0},
        compiler_params=pltpu.CompilerParams(collective_id=0, has_side_effects=True),
        name="gather",
    )(blocks)


def fisher_kernel(group, labels_ref, me_ref, left_ref, right_ref, out_ref, pair):
    step = pl.program_id(0)
    subjects, width, frames = left_ref.shape
    own = labels_ref[me_ref[0]]
    first = labels_ref[2 * step] == own
    second = labels_ref[2 * step + 1] == own
    either = jnp.logical_or(first, second)
    tiles, top = width // LANES, frames // 2
    low, high = tiles * LANES, (tiles + 1) * LANES
    bound = LIMIT * frames

    @pl.when(jnp.logical_not(either))
    def _():
        out_ref[...] = jnp.zeros_like(out_ref)

    @pl.when(either)
    def _():
        for s in range(subjects):
            for t in range(tiles):
                rows = slice(t * frames, (t + 1) * frames)
                pair[s, :, t * LANES : (t + 1) * LANES] = right_ref[0, s, rows, :]
                pair[s, :, high + t * LANES : high + (t + 1) * LANES] = right_ref[1, s, rows, :]
            a = right_ref[0, s, tiles * frames :, :].astype(jnp.float32)
            b = right_ref[1, s, tiles * frames :, :].astype(jnp.float32)
            front = lax.broadcasted_iota(jnp.int32, a.shape, 1) < HALF
            pair[s, :top, low:high] = jnp.where(front, a, b).astype(jnp.bfloat16)
            swapped = pltpu.roll(jnp.where(front, b, a), HALF, 1)
            pair[s, top:, low:high] = swapped.astype(jnp.bfloat16)

    def tile(start, size, wanted, mixed):
        @pl.when(jnp.logical_and(jnp.logical_not(wanted), either))
        def _():
            out_ref[:, start : start + size] = jnp.zeros((width, size), jnp.float32)

        @pl.when(wanted)
        def _():
            total = None
            for g in range(0, subjects, group):
                over = under = None
                for s in range(g, min(g + group, subjects)):
                    dot = jnp.dot(
                        left_ref[s],
                        pair[s, :, start : start + size],
                        preferred_element_type=jnp.float32,
                    )
                    dot = jnp.clip(dot, -bound, bound)
                    plus, minus = frames + dot, frames - dot
                    over = plus if over is None else over * plus
                    under = minus if under is None else under * minus
                term = 0.5 * jnp.log(over / under)
                total = term if total is None else total + term
            if mixed:
                lane = start + lax.broadcasted_iota(jnp.int32, total.shape, 1)
                keep = jnp.where(lane < width, first.astype(jnp.int32), second.astype(jnp.int32))
                total = jnp.where(keep > 0, total, 0.0)
            out_ref[:, start : start + size] = total

    for start in range(0, low, 2 * LANES):
        size = min(2 * LANES, low - start)
        if size < 2 * LANES:
            tile(start, 2 * LANES, either, True)
        else:
            tile(start, size, first, False)
    if tiles % 2 == 0:
        tile(low, LANES, either, True)
    for start in range(high, 2 * width, 2 * LANES):
        tile(start, min(2 * LANES, 2 * width - start), second, False)


def correlate(left, blocks, labels, me):
    count, subjects, depth, _ = blocks.shape
    _, width, frames = left.shape
    pairs = count // 2
    group = max(1, int(30 / math.log10(2 * frames)))

    def fetched(p, labels, me):
        own = labels[me[0]]
        latest = jnp.int32(0)
        for t in range(pairs):
            hit = jnp.logical_or(labels[2 * t] == own, labels[2 * t + 1] == own)
            latest = jnp.where(jnp.logical_and(hit, t <= p), t, latest)
        return latest, 0, 0, 0

    return pl.pallas_call(
        functools.partial(fisher_kernel, group),
        grid_spec=pltpu.PrefetchScalarGridSpec(
            num_scalar_prefetch=2,
            grid=(pairs,),
            in_specs=[
                pl.BlockSpec((subjects, width, frames), lambda p, labels, me: (0, 0, 0)),
                pl.BlockSpec((2, subjects, depth, LANES), fetched),
            ],
            out_specs=pl.BlockSpec((width, 2 * width), lambda p, labels, me: (0, p)),
            scratch_shapes=[pltpu.VMEM((subjects, frames, 2 * width), jnp.bfloat16)],
        ),
        out_shape=jax.ShapeDtypeStruct((width, count * width), jnp.float32),
        compiler_params=pltpu.CompilerParams(vmem_limit_bytes=60 * 1024 * 1024),
        name="correlate",
    )(labels, me, left, blocks)


def on_device(series, subject_ids, net_labels):
    count = lax.axis_size("blk")
    _, frames, width = series.shape
    packs = width % LANES == HALF and frames % 32 == 0
    if not (packs and net_labels.shape[0] == count and count % 4 == 0):
        return plain(series, subject_ids, net_labels)
    me = lax.axis_index("blk").astype(jnp.int32)[None]
    blocks, left = normalized_blocks(series, subject_ids, me, count)
    return correlate(left, gather(blocks, count), net_labels, me)


def solution(mesh):
    return jax.shard_map(
        on_device,
        mesh=mesh,
        in_specs=(P(None, None, "blk"), P("parts"), P()),
        out_specs=P(("parts", "blk"), None),
        check_vma=False,
    )
```

```python
import functools
import math

import jax
import jax.numpy as jnp
from jax import lax
from jax.experimental import pallas as pl
from jax.experimental.pallas import tpu as pltpu
from jax.sharding import PartitionSpec as P

LIMIT = 0.999
LANES = 128
HALF = LANES // 2


def normalize(chosen):
    values = chosen.astype(jnp.float32)
    center = values - jnp.mean(values, axis=1, keepdims=True)
    spread = jnp.mean(center * center, axis=1, keepdims=True)
    return (center / jnp.sqrt(spread + 1e-05)).astype(jnp.bfloat16)


def fisher_sum(left, right):
    frames = left.shape[1]
    total = jnp.zeros((left.shape[2], right.shape[2]), jnp.float32)
    for subject in range(left.shape[0]):
        corr = (
            lax.dot_general(
                left[subject],
                right[subject],
                (((0,), (0,)), ((), ())),
                preferred_element_type=jnp.float32,
            )
            / frames
        )
        clipped = jnp.clip(corr, -LIMIT, LIMIT)
        total = total + 0.5 * jnp.log((1.0 + clipped) / (1.0 - clipped))
    return total


def plain(series, subject_ids, net_labels):
    normalized = normalize(jnp.take(series, subject_ids, axis=0))
    rows = normalized.shape[2]
    index = lax.axis_index("blk")
    count = lax.axis_size("blk")
    row_labels = jnp.repeat(net_labels, count * rows // net_labels.shape[0])
    own_labels = lax.dynamic_slice_in_dim(row_labels, index * rows, rows)
    gathered = lax.all_gather(normalized, "blk", axis=2, tiled=True)
    same = own_labels[:, None] == row_labels[None, :]
    return jnp.where(same, fisher_sum(normalized, gathered), 0.0)


def plan_kernel(ids_ref, list_ref, slot_ref, count_ref):
    subjects = ids_ref.shape[0]
    ids = [ids_ref[s] for s in range(subjects)]
    for s in range(subjects):
        list_ref[s] = ids[0]
    slots, count = [], jnp.int32(0)
    for s in range(subjects):
        slot, fresh = count, jnp.int32(1)
        for earlier in range(s):
            same = ids[earlier] == ids[s]
            slot = jnp.where(same, slots[earlier], slot)
            fresh = jnp.where(same, 0, fresh)
        list_ref[slot] = ids[s]
        slot_ref[s] = slot
        slots.append(slot)
        count = count + fresh
    count_ref[0] = count


def distinct(subject_ids):
    shapes = [subject_ids.shape, subject_ids.shape, (1,)]
    return pl.pallas_call(
        plan_kernel,
        out_shape=[jax.ShapeDtypeStruct(shape, jnp.int32) for shape in shapes],
        in_specs=[pl.BlockSpec(memory_space=pltpu.SMEM)],
        out_specs=[pl.BlockSpec(memory_space=pltpu.SMEM)] * 3,
        name="plan",
    )(subject_ids)


def normalize_kernel(ids_ref, me_ref, series_ref, out_ref, turned_ref):
    values = series_ref[0].astype(jnp.float32)
    frames = values.shape[0]
    center = values - jnp.sum(values, axis=0, keepdims=True) / frames
    spread = jnp.sum(center * center, axis=0, keepdims=True) / frames
    result = center / jnp.sqrt(spread + 1e-05)
    turned_ref[0] = result.T.astype(jnp.bfloat16)
    packed = result.astype(jnp.bfloat16)
    width = packed.shape[1]
    tiles, top = width // LANES, frames // 2

    def pack(first, edge, upper, lower):
        for t in range(tiles):
            start = first + t * LANES
            out_ref[0, 0, t * frames : (t + 1) * frames, :] = packed[:, start : start + LANES]
        ends = {upper: packed[:top, edge : edge + HALF], lower: packed[top:, edge : edge + HALF]}
        out_ref[0, 0, tiles * frames :, :] = jnp.concatenate([ends[0], ends[1]], axis=1)

    pl.when(me_ref[0] % 2 == 0)(lambda: pack(0, tiles * LANES, 0, 1))
    pl.when(me_ref[0] % 2 == 1)(lambda: pack(HALF, 0, 1, 0))


def normalized_blocks(series, subject_ids, me, slots):
    _, frames, width = series.shape
    depth = width * frames // LANES
    subjects = subject_ids.shape[0]
    return pl.pallas_call(
        normalize_kernel,
        grid_spec=pltpu.PrefetchScalarGridSpec(
            num_scalar_prefetch=2,
            grid=(subjects,),
            in_specs=[pl.BlockSpec((1, frames, width), lambda s, ids, me: (ids[s], 0, 0))],
            out_specs=[
                pl.BlockSpec((1, 1, depth, LANES), lambda s, ids, me: (me[0], s, 0, 0)),
                pl.BlockSpec((1, width, frames), lambda s, ids, me: (s, 0, 0)),
            ],
        ),
        out_shape=[
            jax.ShapeDtypeStruct((slots, subjects, depth, LANES), jnp.bfloat16),
            jax.ShapeDtypeStruct((subjects, width, frames), jnp.bfloat16),
        ],
        name="normalize",
    )(subject_ids, me, series)


def gather_kernel(count, sizes, half, in_ref, out_ref, send_sem, recv_sem):
    tall = count // 4
    me = lax.axis_index("blk")
    z = me // 4
    x = (me // 2) % 2
    c = me % 2
    chunks = len(sizes)
    starts = [sum(sizes[:q]) for q in range(chunks)]
    UP, DOWN, SIDE, TWIN = range(4)

    def device(zz, xx, cc):
        return (zz * 2 + xx) * 2 + cc

    target = {
        UP: device(jnp.minimum(z + 1, tall - 1), x, c),
        DOWN: device(jnp.maximum(z - 1, 0), x, c),
        SIDE: device(z, 1 - x, c),
        TWIN: device(z, x, 1 - c),
    }
    has_up, has_down = z + 1 < tall, z > 0

    barrier = pltpu.get_barrier_semaphore()

    def greet(way):
        pl.semaphore_signal(
            barrier, inc=1, device_id={"blk": target[way]}, device_id_type=pl.DeviceIdType.MESH
        )

    greet(SIDE)
    greet(TWIN)
    pl.when(has_up)(lambda: greet(UP))
    pl.when(has_down)(lambda: greet(DOWN))
    pl.semaphore_wait(barrier, 2 + has_up.astype(jnp.int32) + has_down.astype(jnp.int32))

    def copy(way, block, q):
        part = out_ref.at[block, pl.ds(starts[q], sizes[q])]
        return pltpu.make_async_remote_copy(
            src_ref=part,
            dst_ref=part,
            send_sem=send_sem.at[way, block, q],
            recv_sem=recv_sem.at[block, q],
            device_id={"blk": target[way]},
            device_id_type=pl.DeviceIdType.MESH,
        )

    def send(way, block, q):
        copy(way, block, q).start()

    def arrived(block, q):
        copy(TWIN, block, q).wait_recv()

    def by_side(zz, at, q):
        if q < half:
            return jnp.bool_(True)
        low = jnp.logical_and(zz == 0, at > 0)
        high = jnp.logical_and(zz == tall - 1, at < tall - 1)
        return jnp.logical_not(jnp.logical_or(low, high))

    for q in range(chunks):
        pl.when(has_up)(lambda: send(UP, me, q))
        pl.when(has_down)(lambda: send(DOWN, me, q))
        pl.when(by_side(z, z, q))(lambda: send(SIDE, me, q))
        send(TWIN, me, q)

    def step(k, carry):
        for q in range(chunks):

            @pl.when(z - k >= 0)
            def _():
                block = device(z - k, x, c)
                arrived(block, q)
                pl.when(has_up)(lambda: send(UP, block, q))
                pl.when(by_side(z - k, z, q))(lambda: send(SIDE, block, q))
                send(TWIN, block, q)

            @pl.when(z + k < tall)
            def _():
                block = device(z + k, x, c)
                arrived(block, q)
                pl.when(has_down)(lambda: send(DOWN, block, q))
                pl.when(by_side(z + k, z, q))(lambda: send(SIDE, block, q))
                send(TWIN, block, q)

            if q >= half:

                @pl.when(jnp.logical_and(z - k == -1, has_down))
                def _():
                    block = device(0, 1 - x, c)
                    arrived(block, q)
                    pl.when(has_up)(lambda: send(UP, block, q))
                    send(TWIN, block, q)

                @pl.when(jnp.logical_and(z + k == tall, has_up))
                def _():
                    block = device(tall - 1, 1 - x, c)
                    arrived(block, q)
                    pl.when(has_down)(lambda: send(DOWN, block, q))
                    send(TWIN, block, q)

            @pl.when(k == 1)
            def _():
                block = device(z, 1 - x, c)
                arrived(block, q)
                if q >= half:
                    pl.when(jnp.logical_and(z == 0, has_up))(lambda: send(UP, block, q))
                    pl.when(jnp.logical_and(z == tall - 1, has_down))(lambda: send(DOWN, block, q))
                send(TWIN, block, q)

            low = z - k + 1

            @pl.when(jnp.logical_and(jnp.logical_and(k > 1, low >= 0), by_side(low, z, q)))
            def _():
                block = device(low, 1 - x, c)
                arrived(block, q)
                send(TWIN, block, q)

            high = z + k - 1

            @pl.when(jnp.logical_and(jnp.logical_and(k > 1, high < tall), by_side(high, z, q)))
            def _():
                block = device(high, 1 - x, c)
                arrived(block, q)
                send(TWIN, block, q)

        return carry

    lax.fori_loop(1, tall + 1, step, 0)

    def finish(zz, carry):
        for q in range(chunks):
            own = device(zz, x, c)
            other = device(zz, 1 - x, c)
            arrived(device(zz, x, 1 - c), q)
            arrived(device(zz, 1 - x, 1 - c), q)
            copy(TWIN, own, q).wait_send()
            copy(TWIN, other, q).wait_send()
            pl.when(by_side(zz, z, q))(lambda: copy(SIDE, own, q).wait_send())
            pl.when(jnp.logical_and(has_up, zz <= z))(lambda: copy(UP, own, q).wait_send())
            pl.when(jnp.logical_and(has_down, zz >= z))(lambda: copy(DOWN, own, q).wait_send())
            if q >= half:
                pl.when(jnp.logical_and(has_up, zz == 0))(
                    lambda: copy(UP, other, q).wait_send()
                )
                pl.when(jnp.logical_and(has_down, zz == tall - 1))(
                    lambda: copy(DOWN, other, q).wait_send()
                )
        return carry

    lax.fori_loop(0, tall, finish, 0)


def chunk_sizes(slots):
    early = slots - slots // 2
    halves = [[early - early // 2, early // 2], [slots // 2 - slots // 4, slots // 4]]
    return [[size for size in half if size] for half in halves]


def gather(blocks, count, slots, collective_id):
    early, late = chunk_sizes(slots)
    sizes = early + late
    return pl.pallas_call(
        functools.partial(gather_kernel, count, sizes, len(early)),
        out_shape=jax.ShapeDtypeStruct(blocks.shape, blocks.dtype),
        in_specs=[pl.BlockSpec(memory_space=pl.ANY)],
        out_specs=pl.BlockSpec(memory_space=pl.ANY),
        scratch_shapes=[
            pltpu.SemaphoreType.DMA((4, count, len(sizes))),
            pltpu.SemaphoreType.DMA((count, len(sizes))),
        ],
        input_output_aliases={0: 0},
        compiler_params=pltpu.CompilerParams(
            collective_id=collective_id, has_side_effects=True
        ),
        name=f"gather_{slots}",
    )(blocks)


def fisher_kernel(group, labels_ref, me_ref, slot_ref, left_ref, right_ref, out_ref, pair):
    step = pl.program_id(0)
    subjects, width, frames = left_ref.shape
    own = labels_ref[me_ref[0]]
    first = labels_ref[2 * step] == own
    second = labels_ref[2 * step + 1] == own
    either = jnp.logical_or(first, second)
    tiles, top = width // LANES, frames // 2
    low, high = tiles * LANES, (tiles + 1) * LANES
    bound = LIMIT * frames

    @pl.when(jnp.logical_not(either))
    def _():
        out_ref[...] = jnp.zeros_like(out_ref)

    @pl.when(either)
    def _():
        for s in range(subjects):
            for t in range(tiles):
                rows = slice(t * frames, (t + 1) * frames)
                pair[s, :, t * LANES : (t + 1) * LANES] = right_ref[0, s, rows, :]
                pair[s, :, high + t * LANES : high + (t + 1) * LANES] = right_ref[1, s, rows, :]
            a = right_ref[0, s, tiles * frames :, :].astype(jnp.float32)
            b = right_ref[1, s, tiles * frames :, :].astype(jnp.float32)
            front = lax.broadcasted_iota(jnp.int32, a.shape, 1) < HALF
            pair[s, :top, low:high] = jnp.where(front, a, b).astype(jnp.bfloat16)
            swapped = pltpu.roll(jnp.where(front, b, a), HALF, 1)
            pair[s, top:, low:high] = swapped.astype(jnp.bfloat16)

    def tile(start, size, wanted, mixed):
        @pl.when(jnp.logical_and(jnp.logical_not(wanted), either))
        def _():
            out_ref[:, start : start + size] = jnp.zeros((width, size), jnp.float32)

        @pl.when(wanted)
        def _():
            total = None
            for g in range(0, subjects, group):
                over = under = None
                for s in range(g, min(g + group, subjects)):
                    dot = jnp.dot(
                        left_ref[slot_ref[s]],
                        pair[slot_ref[s], :, start : start + size],
                        preferred_element_type=jnp.float32,
                    )
                    dot = jnp.clip(dot, -bound, bound)
                    plus, minus = frames + dot, frames - dot
                    over = plus if over is None else over * plus
                    under = minus if under is None else under * minus
                term = 0.5 * jnp.log(over / under)
                total = term if total is None else total + term
            if mixed:
                lane = start + lax.broadcasted_iota(jnp.int32, total.shape, 1)
                keep = jnp.where(lane < width, first.astype(jnp.int32), second.astype(jnp.int32))
                total = jnp.where(keep > 0, total, 0.0)
            out_ref[:, start : start + size] = total

    for start in range(0, low, 2 * LANES):
        size = min(2 * LANES, low - start)
        if size < 2 * LANES:
            tile(start, 2 * LANES, either, True)
        else:
            tile(start, size, first, False)
    if tiles % 2 == 0:
        tile(low, LANES, either, True)
    for start in range(high, 2 * width, 2 * LANES):
        tile(start, min(2 * LANES, 2 * width - start), second, False)


def correlate(left, blocks, labels, me, slot):
    count, subjects, depth, _ = blocks.shape
    _, width, frames = left.shape
    pairs = count // 2
    group = max(1, int(30 / math.log10(2 * frames)))

    def fetched(p, labels, me, slot):
        own = labels[me[0]]
        latest = jnp.int32(0)
        for t in range(pairs):
            hit = jnp.logical_or(labels[2 * t] == own, labels[2 * t + 1] == own)
            latest = jnp.where(jnp.logical_and(hit, t <= p), t, latest)
        return latest, 0, 0, 0

    return pl.pallas_call(
        functools.partial(fisher_kernel, group),
        grid_spec=pltpu.PrefetchScalarGridSpec(
            num_scalar_prefetch=3,
            grid=(pairs,),
            in_specs=[
                pl.BlockSpec((subjects, width, frames), lambda p, labels, me, slot: (0, 0, 0)),
                pl.BlockSpec((2, subjects, depth, LANES), fetched),
            ],
            out_specs=pl.BlockSpec((width, 2 * width), lambda p, labels, me, slot: (0, p)),
            scratch_shapes=[pltpu.VMEM((subjects, frames, 2 * width), jnp.bfloat16)],
        ),
        out_shape=jax.ShapeDtypeStruct((width, count * width), jnp.float32),
        compiler_params=pltpu.CompilerParams(vmem_limit_bytes=60 * 1024 * 1024),
        name="correlate",
    )(labels, me, slot, left, blocks)


def on_device(series, subject_ids, net_labels):
    count = lax.axis_size("blk")
    _, frames, width = series.shape
    packs = width % LANES == HALF and frames % 32 == 0
    if not (packs and net_labels.shape[0] == count and count % 4 == 0):
        return plain(series, subject_ids, net_labels)
    me = lax.axis_index("blk").astype(jnp.int32)[None]
    subjects = subject_ids.shape[0]
    listed, slot, number = distinct(subject_ids)
    groups = lax.axis_size("parts")
    most = number
    for shift in range(1, groups):
        ring = [(part, (part + shift) % groups) for part in range(groups)]
        most = jnp.maximum(most, lax.ppermute(number, "parts", ring))
    blocks, left = normalized_blocks(series, listed, me, count)
    widths = [subjects - less for less in range(3) if less < subjects]
    runs = [functools.partial(gather, count=count, slots=w, collective_id=i) for i, w in enumerate(widths)]
    spare = jnp.minimum(subjects - most[0], len(widths) - 1)
    blocks = lax.switch(spare, runs, blocks)
    return correlate(left, blocks, net_labels, me, slot)


def solution(mesh):
    return jax.shard_map(
        on_device,
        mesh=mesh,
        in_specs=(P(None, None, "blk"), P("parts"), P()),
        out_specs=P(("parts", "blk"), None),
        check_vma=False,
    )
```

```python
import functools
import math

import jax
import jax.numpy as jnp
from jax import lax
from jax.experimental import pallas as pl
from jax.experimental.pallas import tpu as pltpu
from jax.sharding import PartitionSpec as P

LIMIT = 0.999
LANES = 128
HALF = LANES // 2


def normalize(chosen):
    values = chosen.astype(jnp.float32)
    center = values - jnp.mean(values, axis=1, keepdims=True)
    spread = jnp.mean(center * center, axis=1, keepdims=True)
    return (center / jnp.sqrt(spread + 1e-05)).astype(jnp.bfloat16)


def fisher_sum(left, right):
    frames = left.shape[1]
    total = jnp.zeros((left.shape[2], right.shape[2]), jnp.float32)
    for subject in range(left.shape[0]):
        corr = (
            lax.dot_general(
                left[subject],
                right[subject],
                (((0,), (0,)), ((), ())),
                preferred_element_type=jnp.float32,
            )
            / frames
        )
        clipped = jnp.clip(corr, -LIMIT, LIMIT)
        total = total + 0.5 * jnp.log((1.0 + clipped) / (1.0 - clipped))
    return total


def plain(series, subject_ids, net_labels):
    normalized = normalize(jnp.take(series, subject_ids, axis=0))
    rows = normalized.shape[2]
    index = lax.axis_index("blk")
    count = lax.axis_size("blk")
    row_labels = jnp.repeat(net_labels, count * rows // net_labels.shape[0])
    own_labels = lax.dynamic_slice_in_dim(row_labels, index * rows, rows)
    gathered = lax.all_gather(normalized, "blk", axis=2, tiled=True)
    same = own_labels[:, None] == row_labels[None, :]
    return jnp.where(same, fisher_sum(normalized, gathered), 0.0)


def plan_kernel(ids_ref, list_ref, slot_ref, count_ref):
    subjects = ids_ref.shape[0]
    ids = [ids_ref[s] for s in range(subjects)]
    for s in range(subjects):
        list_ref[s] = ids[0]
    slots, count = [], jnp.int32(0)
    for s in range(subjects):
        slot, fresh = count, jnp.int32(1)
        for earlier in range(s):
            same = ids[earlier] == ids[s]
            slot = jnp.where(same, slots[earlier], slot)
            fresh = jnp.where(same, 0, fresh)
        list_ref[slot] = ids[s]
        slot_ref[s] = slot
        slots.append(slot)
        count = count + fresh
    count_ref[0] = count


def distinct(subject_ids):
    shapes = [subject_ids.shape, subject_ids.shape, (1,)]
    return pl.pallas_call(
        plan_kernel,
        out_shape=[jax.ShapeDtypeStruct(shape, jnp.int32) for shape in shapes],
        in_specs=[pl.BlockSpec(memory_space=pltpu.SMEM)],
        out_specs=[pl.BlockSpec(memory_space=pltpu.SMEM)] * 3,
        name="plan",
    )(subject_ids)


def normalize_kernel(ids_ref, me_ref, series_ref, out_ref, turned_ref):
    values = series_ref[0].astype(jnp.float32)
    frames = values.shape[0]
    center = values - jnp.sum(values, axis=0, keepdims=True) / frames
    spread = jnp.sum(center * center, axis=0, keepdims=True) / frames
    result = center / jnp.sqrt(spread + 1e-05)
    turned_ref[0] = result.T.astype(jnp.bfloat16)
    packed = result.astype(jnp.bfloat16)
    width = packed.shape[1]
    tiles, top = width // LANES, frames // 2

    def pack(first, edge, upper, lower):
        for t in range(tiles):
            start = first + t * LANES
            out_ref[0, 0, t * frames : (t + 1) * frames, :] = packed[:, start : start + LANES]
        ends = {upper: packed[:top, edge : edge + HALF], lower: packed[top:, edge : edge + HALF]}
        out_ref[0, 0, tiles * frames :, :] = jnp.concatenate([ends[0], ends[1]], axis=1)

    pl.when(me_ref[0] % 2 == 0)(lambda: pack(0, tiles * LANES, 0, 1))
    pl.when(me_ref[0] % 2 == 1)(lambda: pack(HALF, 0, 1, 0))


def normalized_blocks(series, subject_ids, me, slots):
    _, frames, width = series.shape
    depth = width * frames // LANES
    subjects = subject_ids.shape[0]
    return pl.pallas_call(
        normalize_kernel,
        grid_spec=pltpu.PrefetchScalarGridSpec(
            num_scalar_prefetch=2,
            grid=(subjects,),
            in_specs=[pl.BlockSpec((1, frames, width), lambda s, ids, me: (ids[s], 0, 0))],
            out_specs=[
                pl.BlockSpec((1, 1, depth, LANES), lambda s, ids, me: (me[0], s, 0, 0)),
                pl.BlockSpec((1, width, frames), lambda s, ids, me: (s, 0, 0)),
            ],
        ),
        out_shape=[
            jax.ShapeDtypeStruct((slots, subjects, depth, LANES), jnp.bfloat16),
            jax.ShapeDtypeStruct((subjects, width, frames), jnp.bfloat16),
        ],
        name="normalize",
    )(subject_ids, me, series)


def gather_kernel(count, sizes, half, in_ref, out_ref, send_sem, recv_sem):
    tall = count // 4
    me = lax.axis_index("blk")
    z = me // 4
    x = (me // 2) % 2
    c = me % 2
    chunks = len(sizes)
    starts = [sum(sizes[:q]) for q in range(chunks)]
    UP, DOWN, SIDE, TWIN = range(4)

    def device(zz, xx, cc):
        return (zz * 2 + xx) * 2 + cc

    target = {
        UP: device(jnp.minimum(z + 1, tall - 1), x, c),
        DOWN: device(jnp.maximum(z - 1, 0), x, c),
        SIDE: device(z, 1 - x, c),
        TWIN: device(z, x, 1 - c),
    }
    has_up, has_down = z + 1 < tall, z > 0

    barrier = pltpu.get_barrier_semaphore()

    def greet(way):
        pl.semaphore_signal(
            barrier, inc=1, device_id={"blk": target[way]}, device_id_type=pl.DeviceIdType.MESH
        )

    greet(SIDE)
    greet(TWIN)
    pl.when(has_up)(lambda: greet(UP))
    pl.when(has_down)(lambda: greet(DOWN))
    pl.semaphore_wait(barrier, 2 + has_up.astype(jnp.int32) + has_down.astype(jnp.int32))

    def copy(way, block, q):
        part = out_ref.at[block, pl.ds(starts[q], sizes[q])]
        return pltpu.make_async_remote_copy(
            src_ref=part,
            dst_ref=part,
            send_sem=send_sem.at[way, block, q],
            recv_sem=recv_sem.at[block, q],
            device_id={"blk": target[way]},
            device_id_type=pl.DeviceIdType.MESH,
        )

    def send(way, block, q):
        copy(way, block, q).start()

    def arrived(block, q):
        copy(TWIN, block, q).wait_recv()

    def by_side(zz, at, q):
        if q < half:
            return jnp.bool_(True)
        low = jnp.logical_and(zz == 0, at > 0)
        high = jnp.logical_and(zz == tall - 1, at < tall - 1)
        return jnp.logical_not(jnp.logical_or(low, high))

    for q in range(chunks):
        pl.when(has_up)(lambda: send(UP, me, q))
        pl.when(has_down)(lambda: send(DOWN, me, q))
        pl.when(by_side(z, z, q))(lambda: send(SIDE, me, q))
        send(TWIN, me, q)

    def step(k, carry):
        for q in range(chunks):

            @pl.when(z - k >= 0)
            def _():
                block = device(z - k, x, c)
                arrived(block, q)
                pl.when(has_up)(lambda: send(UP, block, q))
                pl.when(by_side(z - k, z, q))(lambda: send(SIDE, block, q))
                send(TWIN, block, q)

            @pl.when(z + k < tall)
            def _():
                block = device(z + k, x, c)
                arrived(block, q)
                pl.when(has_down)(lambda: send(DOWN, block, q))
                pl.when(by_side(z + k, z, q))(lambda: send(SIDE, block, q))
                send(TWIN, block, q)

            if q >= half:

                @pl.when(jnp.logical_and(z - k == -1, has_down))
                def _():
                    block = device(0, 1 - x, c)
                    arrived(block, q)
                    pl.when(has_up)(lambda: send(UP, block, q))
                    send(TWIN, block, q)

                @pl.when(jnp.logical_and(z + k == tall, has_up))
                def _():
                    block = device(tall - 1, 1 - x, c)
                    arrived(block, q)
                    pl.when(has_down)(lambda: send(DOWN, block, q))
                    send(TWIN, block, q)

            @pl.when(k == 1)
            def _():
                block = device(z, 1 - x, c)
                arrived(block, q)
                if q >= half:
                    pl.when(jnp.logical_and(z == 0, has_up))(lambda: send(UP, block, q))
                    pl.when(jnp.logical_and(z == tall - 1, has_down))(lambda: send(DOWN, block, q))
                send(TWIN, block, q)

            low = z - k + 1

            @pl.when(jnp.logical_and(jnp.logical_and(k > 1, low >= 0), by_side(low, z, q)))
            def _():
                block = device(low, 1 - x, c)
                arrived(block, q)
                send(TWIN, block, q)

            high = z + k - 1

            @pl.when(jnp.logical_and(jnp.logical_and(k > 1, high < tall), by_side(high, z, q)))
            def _():
                block = device(high, 1 - x, c)
                arrived(block, q)
                send(TWIN, block, q)

        return carry

    lax.fori_loop(1, tall + 1, step, 0)

    def finish(zz, carry):
        for q in range(chunks):
            own = device(zz, x, c)
            other = device(zz, 1 - x, c)
            arrived(device(zz, x, 1 - c), q)
            arrived(device(zz, 1 - x, 1 - c), q)
            copy(TWIN, own, q).wait_send()
            copy(TWIN, other, q).wait_send()
            pl.when(by_side(zz, z, q))(lambda: copy(SIDE, own, q).wait_send())
            pl.when(jnp.logical_and(has_up, zz <= z))(lambda: copy(UP, own, q).wait_send())
            pl.when(jnp.logical_and(has_down, zz >= z))(lambda: copy(DOWN, own, q).wait_send())
            if q >= half:
                pl.when(jnp.logical_and(has_up, zz == 0))(
                    lambda: copy(UP, other, q).wait_send()
                )
                pl.when(jnp.logical_and(has_down, zz == tall - 1))(
                    lambda: copy(DOWN, other, q).wait_send()
                )
        return carry

    lax.fori_loop(0, tall, finish, 0)


def chunk_sizes(slots):
    return [1] * (slots - slots // 2), [1] * (slots // 2)


def gather(blocks, count, slots, collective_id):
    early, late = chunk_sizes(slots)
    sizes = early + late
    return pl.pallas_call(
        functools.partial(gather_kernel, count, sizes, len(early)),
        out_shape=jax.ShapeDtypeStruct(blocks.shape, blocks.dtype),
        in_specs=[pl.BlockSpec(memory_space=pl.ANY)],
        out_specs=pl.BlockSpec(memory_space=pl.ANY),
        scratch_shapes=[
            pltpu.SemaphoreType.DMA((4, count, len(sizes))),
            pltpu.SemaphoreType.DMA((count, len(sizes))),
        ],
        input_output_aliases={0: 0},
        compiler_params=pltpu.CompilerParams(
            collective_id=collective_id, has_side_effects=True
        ),
        name=f"gather_{slots}",
    )(blocks)


def fisher_kernel(group, labels_ref, me_ref, slot_ref, left_ref, right_ref, out_ref, pair):
    step = pl.program_id(0)
    subjects, width, frames = left_ref.shape
    own = labels_ref[me_ref[0]]
    first = labels_ref[2 * step] == own
    second = labels_ref[2 * step + 1] == own
    either = jnp.logical_or(first, second)
    tiles, top = width // LANES, frames // 2
    low, high = tiles * LANES, (tiles + 1) * LANES
    bound = LIMIT * frames

    @pl.when(jnp.logical_not(either))
    def _():
        out_ref[...] = jnp.zeros_like(out_ref)

    @pl.when(either)
    def _():
        for s in range(subjects):
            for t in range(tiles):
                rows = slice(t * frames, (t + 1) * frames)
                pair[s, :, t * LANES : (t + 1) * LANES] = right_ref[0, s, rows, :]
                pair[s, :, high + t * LANES : high + (t + 1) * LANES] = right_ref[1, s, rows, :]
            a = right_ref[0, s, tiles * frames :, :].astype(jnp.float32)
            b = right_ref[1, s, tiles * frames :, :].astype(jnp.float32)
            front = lax.broadcasted_iota(jnp.int32, a.shape, 1) < HALF
            pair[s, :top, low:high] = jnp.where(front, a, b).astype(jnp.bfloat16)
            swapped = pltpu.roll(jnp.where(front, b, a), HALF, 1)
            pair[s, top:, low:high] = swapped.astype(jnp.bfloat16)

    def tile(start, size, wanted, mixed):
        @pl.when(jnp.logical_and(jnp.logical_not(wanted), either))
        def _():
            out_ref[:, start : start + size] = jnp.zeros((width, size), jnp.float32)

        @pl.when(wanted)
        def _():
            total = None
            for g in range(0, subjects, group):
                over = under = None
                for s in range(g, min(g + group, subjects)):
                    dot = jnp.dot(
                        left_ref[slot_ref[s]],
                        pair[slot_ref[s], :, start : start + size],
                        preferred_element_type=jnp.float32,
                    )
                    dot = jnp.clip(dot, -bound, bound)
                    plus, minus = frames + dot, frames - dot
                    over = plus if over is None else over * plus
                    under = minus if under is None else under * minus
                term = 0.5 * jnp.log(over / under)
                total = term if total is None else total + term
            if mixed:
                lane = start + lax.broadcasted_iota(jnp.int32, total.shape, 1)
                keep = jnp.where(lane < width, first.astype(jnp.int32), second.astype(jnp.int32))
                total = jnp.where(keep > 0, total, 0.0)
            out_ref[:, start : start + size] = total

    for start in range(0, low, 2 * LANES):
        size = min(2 * LANES, low - start)
        if size < 2 * LANES:
            tile(start, 2 * LANES, either, True)
        else:
            tile(start, size, first, False)
    if tiles % 2 == 0:
        tile(low, LANES, either, True)
    for start in range(high, 2 * width, 2 * LANES):
        tile(start, min(2 * LANES, 2 * width - start), second, False)


def correlate(left, blocks, labels, me, slot):
    count, subjects, depth, _ = blocks.shape
    _, width, frames = left.shape
    pairs = count // 2
    group = max(1, int(30 / math.log10(2 * frames)))

    def fetched(p, labels, me, slot):
        own = labels[me[0]]
        latest = jnp.int32(0)
        for t in range(pairs):
            hit = jnp.logical_or(labels[2 * t] == own, labels[2 * t + 1] == own)
            latest = jnp.where(jnp.logical_and(hit, t <= p), t, latest)
        return latest, 0, 0, 0

    return pl.pallas_call(
        functools.partial(fisher_kernel, group),
        grid_spec=pltpu.PrefetchScalarGridSpec(
            num_scalar_prefetch=3,
            grid=(pairs,),
            in_specs=[
                pl.BlockSpec((subjects, width, frames), lambda p, labels, me, slot: (0, 0, 0)),
                pl.BlockSpec((2, subjects, depth, LANES), fetched),
            ],
            out_specs=pl.BlockSpec((width, 2 * width), lambda p, labels, me, slot: (0, p)),
            scratch_shapes=[pltpu.VMEM((subjects, frames, 2 * width), jnp.bfloat16)],
        ),
        out_shape=jax.ShapeDtypeStruct((width, count * width), jnp.float32),
        compiler_params=pltpu.CompilerParams(vmem_limit_bytes=60 * 1024 * 1024),
        name="correlate",
    )(labels, me, slot, left, blocks)


def on_device(series, subject_ids, net_labels):
    count = lax.axis_size("blk")
    _, frames, width = series.shape
    packs = width % LANES == HALF and frames % 32 == 0
    if not (packs and net_labels.shape[0] == count and count % 4 == 0):
        return plain(series, subject_ids, net_labels)
    me = lax.axis_index("blk").astype(jnp.int32)[None]
    subjects = subject_ids.shape[0]
    listed, slot, number = distinct(subject_ids)
    groups = lax.axis_size("parts")
    most = number
    for shift in range(1, groups):
        ring = [(part, (part + shift) % groups) for part in range(groups)]
        most = jnp.maximum(most, lax.ppermute(number, "parts", ring))
    blocks, left = normalized_blocks(series, listed, me, count)
    widths = [subjects - less for less in range(3) if less < subjects]
    runs = [functools.partial(gather, count=count, slots=w, collective_id=i) for i, w in enumerate(widths)]
    spare = jnp.minimum(subjects - most[0], len(widths) - 1)
    blocks = lax.switch(spare, runs, blocks)
    return correlate(left, blocks, net_labels, me, slot)


def solution(mesh):
    return jax.shard_map(
        on_device,
        mesh=mesh,
        in_specs=(P(None, None, "blk"), P("parts"), P()),
        out_specs=P(("parts", "blk"), None),
        check_vma=False,
    )
```

```python
import functools
import math

import jax
import jax.numpy as jnp
from jax import lax
from jax.experimental import pallas as pl
from jax.experimental.pallas import tpu as pltpu
from jax.sharding import PartitionSpec as P

LIMIT = 0.999
LANES = 128
HALF = LANES // 2


def normalize(chosen):
    values = chosen.astype(jnp.float32)
    center = values - jnp.mean(values, axis=1, keepdims=True)
    spread = jnp.mean(center * center, axis=1, keepdims=True)
    return (center / jnp.sqrt(spread + 1e-05)).astype(jnp.bfloat16)


def fisher_sum(left, right):
    frames = left.shape[1]
    total = jnp.zeros((left.shape[2], right.shape[2]), jnp.float32)
    for subject in range(left.shape[0]):
        corr = (
            lax.dot_general(
                left[subject],
                right[subject],
                (((0,), (0,)), ((), ())),
                preferred_element_type=jnp.float32,
            )
            / frames
        )
        clipped = jnp.clip(corr, -LIMIT, LIMIT)
        total = total + 0.5 * jnp.log((1.0 + clipped) / (1.0 - clipped))
    return total


def plain(series, subject_ids, net_labels):
    normalized = normalize(jnp.take(series, subject_ids, axis=0))
    rows = normalized.shape[2]
    index = lax.axis_index("blk")
    count = lax.axis_size("blk")
    row_labels = jnp.repeat(net_labels, count * rows // net_labels.shape[0])
    own_labels = lax.dynamic_slice_in_dim(row_labels, index * rows, rows)
    gathered = lax.all_gather(normalized, "blk", axis=2, tiled=True)
    same = own_labels[:, None] == row_labels[None, :]
    return jnp.where(same, fisher_sum(normalized, gathered), 0.0)


def plan_kernel(ids_ref, list_ref, slot_ref, count_ref):
    subjects = ids_ref.shape[0]
    ids = [ids_ref[s] for s in range(subjects)]
    for s in range(subjects):
        list_ref[s] = ids[0]
    slots, count = [], jnp.int32(0)
    for s in range(subjects):
        slot, fresh = count, jnp.int32(1)
        for earlier in range(s):
            same = ids[earlier] == ids[s]
            slot = jnp.where(same, slots[earlier], slot)
            fresh = jnp.where(same, 0, fresh)
        list_ref[slot] = ids[s]
        slot_ref[s] = slot
        slots.append(slot)
        count = count + fresh
    count_ref[0] = count


def distinct(subject_ids):
    shapes = [subject_ids.shape, subject_ids.shape, (1,)]
    return pl.pallas_call(
        plan_kernel,
        out_shape=[jax.ShapeDtypeStruct(shape, jnp.int32) for shape in shapes],
        in_specs=[pl.BlockSpec(memory_space=pltpu.SMEM)],
        out_specs=[pl.BlockSpec(memory_space=pltpu.SMEM)] * 3,
        name="plan",
    )(subject_ids)


def normalize_kernel(ids_ref, me_ref, series_ref, out_ref, turned_ref):
    values = series_ref[0].astype(jnp.float32)
    frames = values.shape[0]
    center = values - jnp.sum(values, axis=0, keepdims=True) / frames
    spread = jnp.sum(center * center, axis=0, keepdims=True) / frames
    result = center / jnp.sqrt(spread + 1e-05)
    packed = result.astype(jnp.bfloat16)
    turned_ref[0] = packed.T
    width = packed.shape[1]
    tiles, top = width // LANES, frames // 2

    def pack(first, edge, upper, lower):
        for t in range(tiles):
            start = first + t * LANES
            out_ref[0, 0, t * frames : (t + 1) * frames, :] = packed[:, start : start + LANES]
        ends = {upper: packed[:top, edge : edge + HALF], lower: packed[top:, edge : edge + HALF]}
        out_ref[0, 0, tiles * frames :, :] = jnp.concatenate([ends[0], ends[1]], axis=1)

    pl.when(me_ref[0] % 2 == 0)(lambda: pack(0, tiles * LANES, 0, 1))
    pl.when(me_ref[0] % 2 == 1)(lambda: pack(HALF, 0, 1, 0))


def normalized_blocks(series, subject_ids, me, slots):
    _, frames, width = series.shape
    depth = width * frames // LANES
    subjects = subject_ids.shape[0]
    return pl.pallas_call(
        normalize_kernel,
        grid_spec=pltpu.PrefetchScalarGridSpec(
            num_scalar_prefetch=2,
            grid=(subjects,),
            in_specs=[pl.BlockSpec((1, frames, width), lambda s, ids, me: (ids[s], 0, 0))],
            out_specs=[
                pl.BlockSpec((1, 1, depth, LANES), lambda s, ids, me: (me[0], s, 0, 0)),
                pl.BlockSpec((1, width, frames), lambda s, ids, me: (s, 0, 0)),
            ],
        ),
        out_shape=[
            jax.ShapeDtypeStruct((slots, subjects, depth, LANES), jnp.bfloat16),
            jax.ShapeDtypeStruct((subjects, width, frames), jnp.bfloat16),
        ],
        name="normalize",
    )(subject_ids, me, series)


def gather_kernel(count, sizes, half, in_ref, out_ref, send_sem, recv_sem):
    tall = count // 4
    me = lax.axis_index("blk")
    z = me // 4
    x = (me // 2) % 2
    c = me % 2
    chunks = len(sizes)
    starts = [sum(sizes[:q]) for q in range(chunks)]
    UP, DOWN, SIDE, TWIN = range(4)

    def device(zz, xx, cc):
        return (zz * 2 + xx) * 2 + cc

    target = {
        UP: device(jnp.minimum(z + 1, tall - 1), x, c),
        DOWN: device(jnp.maximum(z - 1, 0), x, c),
        SIDE: device(z, 1 - x, c),
        TWIN: device(z, x, 1 - c),
    }
    has_up, has_down = z + 1 < tall, z > 0

    barrier = pltpu.get_barrier_semaphore()

    def greet(way):
        pl.semaphore_signal(
            barrier, inc=1, device_id={"blk": target[way]}, device_id_type=pl.DeviceIdType.MESH
        )

    greet(SIDE)
    greet(TWIN)
    pl.when(has_up)(lambda: greet(UP))
    pl.when(has_down)(lambda: greet(DOWN))
    pl.semaphore_wait(barrier, 2 + has_up.astype(jnp.int32) + has_down.astype(jnp.int32))

    def copy(way, block, q):
        part = out_ref.at[block, pl.ds(starts[q], sizes[q])]
        return pltpu.make_async_remote_copy(
            src_ref=part,
            dst_ref=part,
            send_sem=send_sem.at[way, block, q],
            recv_sem=recv_sem.at[block, q],
            device_id={"blk": target[way]},
            device_id_type=pl.DeviceIdType.MESH,
        )

    def send(way, block, q):
        copy(way, block, q).start()

    def arrived(block, q):
        copy(TWIN, block, q).wait_recv()

    def by_side(zz, at, q):
        if q < half:
            return jnp.bool_(True)
        low = jnp.logical_and(zz == 0, at > 0)
        high = jnp.logical_and(zz == tall - 1, at < tall - 1)
        return jnp.logical_not(jnp.logical_or(low, high))

    for q in range(chunks):
        pl.when(has_up)(lambda: send(UP, me, q))
        pl.when(has_down)(lambda: send(DOWN, me, q))
        pl.when(by_side(z, z, q))(lambda: send(SIDE, me, q))
        send(TWIN, me, q)

    def step(k, carry):
        for q in range(chunks):

            @pl.when(z - k >= 0)
            def _():
                block = device(z - k, x, c)
                arrived(block, q)
                pl.when(has_up)(lambda: send(UP, block, q))
                pl.when(by_side(z - k, z, q))(lambda: send(SIDE, block, q))
                send(TWIN, block, q)

            @pl.when(z + k < tall)
            def _():
                block = device(z + k, x, c)
                arrived(block, q)
                pl.when(has_down)(lambda: send(DOWN, block, q))
                pl.when(by_side(z + k, z, q))(lambda: send(SIDE, block, q))
                send(TWIN, block, q)

            if q >= half:

                @pl.when(jnp.logical_and(z - k == -1, has_down))
                def _():
                    block = device(0, 1 - x, c)
                    arrived(block, q)
                    pl.when(has_up)(lambda: send(UP, block, q))
                    send(TWIN, block, q)

                @pl.when(jnp.logical_and(z + k == tall, has_up))
                def _():
                    block = device(tall - 1, 1 - x, c)
                    arrived(block, q)
                    pl.when(has_down)(lambda: send(DOWN, block, q))
                    send(TWIN, block, q)

            @pl.when(k == 1)
            def _():
                block = device(z, 1 - x, c)
                arrived(block, q)
                if q >= half:
                    pl.when(jnp.logical_and(z == 0, has_up))(lambda: send(UP, block, q))
                    pl.when(jnp.logical_and(z == tall - 1, has_down))(lambda: send(DOWN, block, q))
                send(TWIN, block, q)

            low = z - k + 1

            @pl.when(jnp.logical_and(jnp.logical_and(k > 1, low >= 0), by_side(low, z, q)))
            def _():
                block = device(low, 1 - x, c)
                arrived(block, q)
                send(TWIN, block, q)

            high = z + k - 1

            @pl.when(jnp.logical_and(jnp.logical_and(k > 1, high < tall), by_side(high, z, q)))
            def _():
                block = device(high, 1 - x, c)
                arrived(block, q)
                send(TWIN, block, q)

        return carry

    lax.fori_loop(1, tall + 1, step, 0)

    def finish(zz, carry):
        for q in range(chunks):
            own = device(zz, x, c)
            other = device(zz, 1 - x, c)
            arrived(device(zz, x, 1 - c), q)
            arrived(device(zz, 1 - x, 1 - c), q)
            copy(TWIN, own, q).wait_send()
            copy(TWIN, other, q).wait_send()
            pl.when(by_side(zz, z, q))(lambda: copy(SIDE, own, q).wait_send())
            pl.when(jnp.logical_and(has_up, zz <= z))(lambda: copy(UP, own, q).wait_send())
            pl.when(jnp.logical_and(has_down, zz >= z))(lambda: copy(DOWN, own, q).wait_send())
            if q >= half:
                pl.when(jnp.logical_and(has_up, zz == 0))(
                    lambda: copy(UP, other, q).wait_send()
                )
                pl.when(jnp.logical_and(has_down, zz == tall - 1))(
                    lambda: copy(DOWN, other, q).wait_send()
                )
        return carry

    lax.fori_loop(0, tall, finish, 0)


def chunk_sizes(slots):
    early = slots - slots // 2
    halves = [[early - early // 2, early // 2], [slots // 2 - slots // 4, slots // 4]]
    return [[size for size in half if size] for half in halves]


def gather(blocks, count, slots, collective_id):
    early, late = chunk_sizes(slots)
    sizes = early + late
    return pl.pallas_call(
        functools.partial(gather_kernel, count, sizes, len(early)),
        out_shape=jax.ShapeDtypeStruct(blocks.shape, blocks.dtype),
        in_specs=[pl.BlockSpec(memory_space=pl.ANY)],
        out_specs=pl.BlockSpec(memory_space=pl.ANY),
        scratch_shapes=[
            pltpu.SemaphoreType.DMA((4, count, len(sizes))),
            pltpu.SemaphoreType.DMA((count, len(sizes))),
        ],
        input_output_aliases={0: 0},
        compiler_params=pltpu.CompilerParams(
            collective_id=collective_id, has_side_effects=True
        ),
        name=f"gather_{slots}",
    )(blocks)


def fisher_kernel(group, labels_ref, me_ref, slot_ref, left_ref, right_ref, out_ref, pair):
    step = pl.program_id(0)
    subjects, width, frames = left_ref.shape
    own = labels_ref[me_ref[0]]
    first = labels_ref[2 * step] == own
    second = labels_ref[2 * step + 1] == own
    either = jnp.logical_or(first, second)
    tiles, top = width // LANES, frames // 2
    low, high = tiles * LANES, (tiles + 1) * LANES
    bound = LIMIT * frames

    @pl.when(jnp.logical_not(either))
    def _():
        out_ref[...] = jnp.zeros_like(out_ref)

    @pl.when(either)
    def _():
        for s in range(subjects):
            for t in range(tiles):
                rows = slice(t * frames, (t + 1) * frames)
                pair[s, :, t * LANES : (t + 1) * LANES] = right_ref[0, s, rows, :]
                pair[s, :, high + t * LANES : high + (t + 1) * LANES] = right_ref[1, s, rows, :]
            a = right_ref[0, s, tiles * frames :, :].astype(jnp.float32)
            b = right_ref[1, s, tiles * frames :, :].astype(jnp.float32)
            front = lax.broadcasted_iota(jnp.int32, a.shape, 1) < HALF
            pair[s, :top, low:high] = jnp.where(front, a, b).astype(jnp.bfloat16)
            swapped = pltpu.roll(jnp.where(front, b, a), HALF, 1)
            pair[s, top:, low:high] = swapped.astype(jnp.bfloat16)

    def tile(start, size, wanted, mixed):
        @pl.when(jnp.logical_and(jnp.logical_not(wanted), either))
        def _():
            out_ref[:, start : start + size] = jnp.zeros((width, size), jnp.float32)

        @pl.when(wanted)
        def _():
            total = None
            for g in range(0, subjects, group):
                over = under = None
                for s in range(g, min(g + group, subjects)):
                    dot = jnp.dot(
                        left_ref[slot_ref[s]],
                        pair[slot_ref[s], :, start : start + size],
                        preferred_element_type=jnp.float32,
                    )
                    dot = jnp.clip(dot, -bound, bound)
                    plus, minus = frames + dot, frames - dot
                    over = plus if over is None else over * plus
                    under = minus if under is None else under * minus
                term = 0.5 * jnp.log(over / under)
                total = term if total is None else total + term
            if mixed:
                lane = start + lax.broadcasted_iota(jnp.int32, total.shape, 1)
                keep = jnp.where(lane < width, first.astype(jnp.int32), second.astype(jnp.int32))
                total = jnp.where(keep > 0, total, 0.0)
            out_ref[:, start : start + size] = total

    for start in range(0, low, 2 * LANES):
        size = min(2 * LANES, low - start)
        if size < 2 * LANES:
            tile(start, 2 * LANES, either, True)
        else:
            tile(start, size, first, False)
    if tiles % 2 == 0:
        tile(low, LANES, either, True)
    for start in range(high, 2 * width, 2 * LANES):
        tile(start, min(2 * LANES, 2 * width - start), second, False)


def correlate(left, blocks, labels, me, slot):
    count, subjects, depth, _ = blocks.shape
    _, width, frames = left.shape
    pairs = count // 2
    group = max(1, int(30 / math.log10(2 * frames)))

    def fetched(p, labels, me, slot):
        own = labels[me[0]]
        latest = jnp.int32(0)
        for t in range(pairs):
            hit = jnp.logical_or(labels[2 * t] == own, labels[2 * t + 1] == own)
            latest = jnp.where(jnp.logical_and(hit, t <= p), t, latest)
        return latest, 0, 0, 0

    return pl.pallas_call(
        functools.partial(fisher_kernel, group),
        grid_spec=pltpu.PrefetchScalarGridSpec(
            num_scalar_prefetch=3,
            grid=(pairs,),
            in_specs=[
                pl.BlockSpec((subjects, width, frames), lambda p, labels, me, slot: (0, 0, 0)),
                pl.BlockSpec((2, subjects, depth, LANES), fetched),
            ],
            out_specs=pl.BlockSpec((width, 2 * width), lambda p, labels, me, slot: (0, p)),
            scratch_shapes=[pltpu.VMEM((subjects, frames, 2 * width), jnp.bfloat16)],
        ),
        out_shape=jax.ShapeDtypeStruct((width, count * width), jnp.float32),
        compiler_params=pltpu.CompilerParams(vmem_limit_bytes=60 * 1024 * 1024),
        name="correlate",
    )(labels, me, slot, left, blocks)


def on_device(series, subject_ids, net_labels):
    count = lax.axis_size("blk")
    _, frames, width = series.shape
    packs = width % LANES == HALF and frames % 32 == 0
    if not (packs and net_labels.shape[0] == count and count % 4 == 0):
        return plain(series, subject_ids, net_labels)
    me = lax.axis_index("blk").astype(jnp.int32)[None]
    subjects = subject_ids.shape[0]
    listed, slot, number = distinct(subject_ids)
    groups = lax.axis_size("parts")
    most = number
    for shift in range(1, groups):
        ring = [(part, (part + shift) % groups) for part in range(groups)]
        most = jnp.maximum(most, lax.ppermute(number, "parts", ring))
    blocks, left = normalized_blocks(series, listed, me, count)
    widths = [subjects - less for less in range(3) if less < subjects]
    runs = [functools.partial(gather, count=count, slots=w, collective_id=i) for i, w in enumerate(widths)]
    spare = jnp.minimum(subjects - most[0], len(widths) - 1)
    blocks = lax.switch(spare, runs, blocks)
    return correlate(left, blocks, net_labels, me, slot)


def solution(mesh):
    return jax.shard_map(
        on_device,
        mesh=mesh,
        in_specs=(P(None, None, "blk"), P("parts"), P()),
        out_specs=P(("parts", "blk"), None),
        check_vma=False,
    )
```
